32 devices in a mesh: wide: 8 (over z, y), narrow: 4 (over x, core).
Axes of the slice: x: 2, y: 2, z: 4, core: 2. Of those that a mesh axis runs over, the one named last changes fastest.
Arguments:
- features: bfloat16 [512, 32768], P('narrow', 'wide'), may hold values from -36 to 36
- edge_tiles: bfloat16 [256, 12, 128, 128], P('wide'), may hold values from 0 to 22, as said below
- block_lists: int32 [256, 12], P('wide'), may hold values from 0 to 47, as said below
- send_lists: int32 [8, 8, 2], P('wide'), may hold values from 0 to 31
- train_ids: int32 [2048], P('wide'), may hold values from 0 to 4095, as said below
- owners: int32 [2048, 1], P('wide'), may hold values from 0 to 31; in each aligned block of 256 rows (0 to 255, 256 to 511, ...) at most 16 rows name the same one
- cotangent: bfloat16 [4, 512, 2048], P(None, 'narrow', 'wide'), may hold values from -6 to 6
- query_weight: bfloat16 [512, 512], replicated, may hold values from -8 to 8
- key_weight: bfloat16 [512, 512], replicated, may hold values from -8 to 8
- value_weight: bfloat16 [512, 512], replicated, may hold values from -0.25 to 0.25
- out_weight: bfloat16 [512, 512], replicated, may hold values from -0.25 to 0.25
- up_weight: bfloat16 [2048, 512], replicated, may hold values from -0.25 to 0.25
- down_weight: bfloat16 [2048, 512], replicated, may hold values from -0.125 to 0.125
Outputs:
- hop_tokens: bfloat16 [3, 512, 32768], P(None, 'narrow', 'wide')
- grad_attn: float32 [2048, 512], P(('wide', 'narrow'))
- grad_up: float32 [2048, 512], P(('wide', 'narrow'))
- grad_down: float32 [2048, 512], P(('wide', 'narrow'))
The draws below stay inside these ranges and needn't reach their ends.
Inputs may be any that keep to these rules, and one draw needn't show every extreme that they name: edge_tiles[b, k, s, t] weighs the edge from node s of block source[b, k] to node t of block b; the diagonal of every edge_tiles[b, 0] is positive. block_lists[b, 0] = b mod 32; within every part each position 32 to 47 appears. `train_ids`: distinct within a part. `owners`: at most 16 of the 256 training nodes of one part name the same owner; every owner is named by some node.
All inputs are finite; a program needn't handle non-finite values.
Results may differ from the reference program's by a relative error of at most 0.025.
Values may be sent and summed in bfloat16 or wider, within the bound.
A program may use at most 128 MiB of HBM per device.

```python
import math
import jax
import jax.numpy as jnp
import numpy as np
from jax import lax

D = 512
FF = 2048
HEADS = 8
HOPS = 3
TOKS = 4
BLK = 128
K = 12
SEND = 2
NB = 32
MB = 128
PARTS_SIZE = 8
NODES_PART = 4096
NODES = 32768
TRAIN_PART = 256
TRAINS = 2048
DEVICES = 32


def draw_features(key, part):
    key_rows, key_cols, key_base = jax.random.split(key, 3)
    row_scale = jnp.exp(jax.random.uniform(key_rows, (D, 1), jnp.float32, math.log(0.3), math.log(3.0)))
    col_scale = jnp.exp(jax.random.uniform(key_cols, (1, NODES), jnp.float32, math.log(0.3), math.log(3.0)))
    base_draw = jnp.clip(jax.random.normal(key_base, (D, NODES), jnp.float32), -4.0, 4.0)
    return (base_draw * row_scale * col_scale).astype(jnp.bfloat16)


def draw_edge_tiles(key, part):
    key_mask, key_weight, key_self = jax.random.split(key, 3)
    tile_shape = (PARTS_SIZE * NB, K, BLK, BLK)
    present = jax.random.uniform(key_mask, tile_shape, jnp.float32) < 0.125
    weight = jnp.exp(jax.random.uniform(key_weight, tile_shape, jnp.float32, math.log(0.05), math.log(20.0)))
    self_loops = jnp.exp(jax.random.uniform(key_self, (PARTS_SIZE * NB, BLK), jnp.float32, math.log(0.5), math.log(2.0)))
    diagonal = jnp.eye(BLK, dtype=jnp.float32)[None] * self_loops[:, None, :]
    tiles_all = jnp.where(present, weight, 0.0)
    tiles_all = tiles_all.at[:, 0].add(diagonal)
    return tiles_all.astype(jnp.bfloat16)


def draw_block_lists(key, part):
    part_keys = jax.random.split(key, PARTS_SIZE)
    ref_count = NB * (K - 1)

    def single_part(sub_key):
        key_refs, key_shuffle = jax.random.split(sub_key, 2)
        random_refs = jax.random.randint(key_refs, (ref_count,), 0, NB + PARTS_SIZE * SEND)
        positions = jnp.arange(ref_count, dtype=jnp.int32)
        forced_refs = NB + positions % (PARTS_SIZE * SEND)
        all_refs = jnp.where(positions < PARTS_SIZE * SEND, forced_refs, random_refs)
        shuffle = jax.random.permutation(key_shuffle, ref_count)
        all_refs = all_refs[shuffle].reshape(NB, K - 1)
        own_refs = jnp.arange(NB, dtype=jnp.int32)[:, None]
        return jnp.concatenate([own_refs, all_refs.astype(jnp.int32)], axis=1)
    return jax.vmap(single_part)(part_keys).reshape(PARTS_SIZE * NB, K).astype(jnp.int32)


def draw_train_ids(key, part):
    part_keys = jax.random.split(key, PARTS_SIZE)

    def single_part(sub_key):
        return jax.random.permutation(sub_key, NODES_PART)[:TRAIN_PART]
    return jax.vmap(single_part)(part_keys).reshape(-1).astype(jnp.int32)


def attention_weight(key, salt_value):
    base_draw = jnp.clip(jax.random.normal(jax.random.fold_in(key, salt_value), (D, D), jnp.float32), -4.0, 4.0) / math.sqrt(D)
    return base_draw.astype(jnp.bfloat16)


def draw_query_weight(key, part):
    return attention_weight(key, 1)


def draw_key_weight(key, part):
    return attention_weight(key, 2)


def touch_ends(entries, rng, low, top_value):
    longest = entries.shape.index(max(entries.shape))
    spots = []
    for shift in (0, 1):
        where = [jax.random.randint(jax.random.fold_in(rng, axis), (), 0, length) for axis, length in enumerate(entries.shape)]
        where[longest] = (where[longest] + shift) % entries.shape[longest]
        spots.append(tuple(where))
    return entries.at[spots[0]].set(low).at[spots[1]].set(top_value)


def steps_of(stream_key, extent, cuts, least, largest):
    gain = 1.0
    for dim, parts in cuts:
        heights = jax.random.uniform(jax.random.fold_in(jax.random.fold_in(stream_key, 6), dim), (parts,), jnp.float32, least / len(cuts), largest / len(cuts))
        gain = gain * jnp.repeat(jnp.exp(heights), extent[dim] // parts).reshape((-1,) + (1,) * (len(extent) - 1 - dim))
    return gain


def shared_out(key, own, number, rows, amount, top, bound, slope):
    order = jax.random.permutation(key, amount)
    packed, common = load_shares(amount, rows * top, bound, slope, True), load_shares(amount, rows * top, bound, slope, False)
    places = jnp.arange(amount)

    def named(sizes, rotation):
        used = int((sizes > 0).sum())
        fixed = max(1, used // 4)
        moved = fixed + (places - fixed + rotation * (used - fixed)) % max(1, amount - fixed)
        return jnp.zeros((amount,), jnp.int32).at[order[jnp.where(places < fixed, places, moved)]].set(jnp.asarray(sizes, jnp.int32))

    sizes = jnp.where(number % 4 == 0, named(packed, number // 4), named(common, number - number // 4 - 1))
    mixed = jax.random.permutation(jax.random.fold_in(own, 3), amount)
    donor, taker = mixed[0:amount // 2 * 2:2], mixed[1:amount // 2 * 2:2]
    room = jnp.minimum(sizes[donor] - 1, bound - sizes[taker]) // 2
    room = jnp.where((donor == order[0]) | (taker == order[0]) | (sizes[taker] == 0), 0, jnp.maximum(room, 0))
    moved = jax.random.randint(jax.random.fold_in(own, 4), (amount // 2,), 0, 1 << 20) % (room + 1)
    sizes = sizes.at[donor].add(-moved).at[taker].add(moved)
    items = jnp.searchsorted(jnp.cumsum(sizes), jnp.arange(rows * top), side="right").astype(jnp.int32)
    table = items.reshape(top, rows).T
    table = table[jax.random.permutation(jax.random.fold_in(own, 1), rows)]
    rotation = jax.random.randint(jax.random.fold_in(own, 2), (rows, 1), 0, top)
    return jnp.take_along_axis(table, (jnp.arange(top)[None, :] + rotation) % top, axis=1)


def load_shares(number_of, total, bound, skew, full):
    weights = [(1 << 20) // math.isqrt(rank ** skew) + 1 for rank in range(1, number_of + 1)]
    largest = bound if full else min(bound, max(-(-total // number_of), total * weights[0] // sum(weights)))
    least = 1 if total - largest >= number_of - 1 else 0
    given, spare = [largest] + [least] * (number_of - 1), total - largest - least * (number_of - 1)
    while spare > 0:
        candidates = [i for i in range(1, number_of) if given[i] < largest] or [i for i in range(1, number_of) if given[i] < bound]
        pool, left = sum([weights[i] for i in candidates]), spare
        for i in candidates:
            extra = min(bound - given[i], max(1, left * weights[i] // pool), spare)
            given[i] = given[i] + extra
            spare = spare - extra
    return np.array(given)


def centred(own_key, dims, spread, limit, pieces=(), held_as=jnp.bfloat16):
    values = jax.random.normal(own_key, dims, jnp.float32) * spread
    if len(pieces) > 0:
        values = steps_of(own_key, dims, pieces, -0.22, 0.18) * values
    return jnp.clip(values, min=-limit, max=limit).astype(held_as)


def setup_inputs(seed: int = 0) -> dict:
    key_of = jax.random.split(jax.random.key(seed), 14)
    features = draw_features(jax.random.fold_in(key_of[13], 71), 0)
    edge_tiles = draw_edge_tiles(jax.random.fold_in(key_of[13], 71), 0)
    block_lists = draw_block_lists(jax.random.fold_in(key_of[13], 71), 0)
    send_lists = touch_ends(jax.random.randint(key_of[3], (PARTS_SIZE, PARTS_SIZE, SEND), 0, NB), jax.random.fold_in(key_of[3], 1), 0, NB - 1).astype(jnp.int32)
    train_ids = draw_train_ids(jax.random.fold_in(key_of[13], 71), 0)
    owners_keys = jax.random.split(jax.random.fold_in(key_of[5], 1), TRAINS // TRAIN_PART)
    owners_turns = jax.random.permutation(jax.random.fold_in(key_of[5], 3), TRAINS // TRAIN_PART)
    owners = jax.vmap(lambda own, number: shared_out(jax.random.fold_in(key_of[5], 2), own, number, TRAIN_PART, DEVICES, 1, MB // PARTS_SIZE, 2))(owners_keys, owners_turns).reshape((TRAINS, 1))
    cotangent = centred(key_of[6], (TOKS, D, TRAINS), 1.0, 6.0, ((1, 4), (2, 8)))
    query_weight = draw_query_weight(jax.random.fold_in(key_of[13], 71), 0)
    key_weight = draw_key_weight(jax.random.fold_in(key_of[13], 71), 0)
    value_weight = centred(key_of[9], (D, D), D ** -0.5, 0.25)
    out_weight = centred(key_of[10], (D, D), D ** -0.5, 0.25)
    up_weight = centred(key_of[11], (FF, D), D ** -0.5, 0.25)
    down_weight = centred(key_of[12], (FF, D), FF ** -0.5, 0.125)
    return {"features": features, "edge_tiles": edge_tiles, "block_lists": block_lists, "send_lists": send_lists, "train_ids": train_ids, "owners": owners, "cotangent": cotangent, "query_weight": query_weight, "key_weight": key_weight, "value_weight": value_weight, "out_weight": out_weight, "up_weight": up_weight, "down_weight": down_weight}


epsilon = 1e-05

def product_of(pattern, first_arg, second_arg):
    return jnp.einsum(pattern, first_arg.astype(jnp.float32), second_arg.astype(jnp.float32))

def normalize(hidden):
    center = hidden - lax.optimization_barrier(jnp.mean(hidden, axis=1, keepdims=True))
    inverse = lax.rsqrt(lax.optimization_barrier(jnp.mean(center * center, axis=1, keepdims=True)) + epsilon)
    return (center * inverse, inverse)

def norm_back(upstream, normed, inverse):
    return inverse * (upstream - lax.optimization_barrier(jnp.mean(upstream, axis=1, keepdims=True)) - normed * lax.optimization_barrier(jnp.mean(upstream * normed, axis=1, keepdims=True)))

def gelu_tanh(values):
    return jax.nn.gelu(values, approximate=True)

def layer_grads(tokens, cotangent, query_weight, key_weight, value_weight, out_weight, up_weight, down_weight):
    tok_count, feat_width, row_count = tokens.shape
    head_dim = feat_width // HEADS
    score_scale = 1.0 / math.sqrt(head_dim)
    split_heads = (tok_count, HEADS, head_dim, row_count)
    first_norm, _ = normalize(tokens.astype(jnp.float32))
    normed_a = first_norm.astype(jnp.bfloat16)
    query_heads = product_of('od,tdr->tor', query_weight, normed_a).astype(jnp.bfloat16).reshape(split_heads)
    key_heads = product_of('od,tdr->tor', key_weight, normed_a).astype(jnp.bfloat16).reshape(split_heads)
    value_heads = product_of('od,tdr->tor', value_weight, normed_a).astype(jnp.bfloat16).reshape(split_heads)
    scores = product_of('thdr,uhdr->htur', query_heads, key_heads) * score_scale
    attn_probs = jax.nn.softmax(scores, axis=2)
    attn_low = attn_probs.astype(jnp.bfloat16)
    mixed_heads = product_of('htur,uhdr->thdr', attn_low, value_heads).astype(jnp.bfloat16).reshape(tok_count, feat_width, row_count)
    residual = (tokens.astype(jnp.float32) + product_of('od,tdr->tor', out_weight, mixed_heads)).astype(jnp.bfloat16)
    second_norm, second_inv = normalize(residual.astype(jnp.float32))
    normed_b = second_norm.astype(jnp.bfloat16)
    pre_act = product_of('fd,tdr->tfr', up_weight, normed_b)
    activated = gelu_tanh(pre_act).astype(jnp.bfloat16)
    sum_down = product_of('tfr,tdr->fd', activated, cotangent)
    grad_act = product_of('fd,tdr->tfr', down_weight, cotangent)
    _, gelu_back = jax.vjp(gelu_tanh, pre_act)
    grad_pre = gelu_back(grad_act)[0].astype(jnp.bfloat16)
    sum_up = product_of('tfr,tdr->fd', grad_pre, normed_b)
    grad_normed = product_of('fd,tfr->tdr', up_weight, grad_pre)
    grad_resid = (cotangent.astype(jnp.float32) + norm_back(grad_normed, second_norm, second_inv)).astype(jnp.bfloat16)
    sum_out = product_of('tor,tdr->od', grad_resid, mixed_heads)
    grad_mixed = product_of('od,tor->tdr', out_weight, grad_resid).astype(jnp.bfloat16).reshape(split_heads)
    grad_probs = product_of('thdr,uhdr->htur', grad_mixed, value_heads)
    grad_value = product_of('htur,thdr->uhdr', attn_low, grad_mixed).astype(jnp.bfloat16)
    grad_scores = (attn_probs * (grad_probs - lax.optimization_barrier(jnp.sum(attn_probs * grad_probs, axis=2, keepdims=True))) * score_scale).astype(jnp.bfloat16)
    grad_query = product_of('htur,uhdr->thdr', grad_scores, key_heads).astype(jnp.bfloat16)
    grad_key = product_of('htur,thdr->uhdr', grad_scores, query_heads).astype(jnp.bfloat16)
    flat_shape = (tok_count, feat_width, row_count)
    sum_query = product_of('tor,tdr->od', grad_query.reshape(flat_shape), normed_a)
    sum_key = product_of('tor,tdr->od', grad_key.reshape(flat_shape), normed_a)
    sum_value = product_of('tor,tdr->od', grad_value.reshape(flat_shape), normed_a)
    return (jnp.concatenate([sum_query, sum_key, sum_value, sum_out], axis=0), sum_up, sum_down)

def global_sources(block_lists, send_lists):
    block_count = block_lists.shape[0]
    home_part = (jnp.arange(block_count, dtype=jnp.int32) // NB)[:, None]
    is_local = block_lists < NB
    halo_slot = jnp.maximum(block_lists - NB, 0)
    peer_part = halo_slot // SEND
    peer_slot = halo_slot % SEND
    remote = peer_part * NB + send_lists[peer_part, home_part, peer_slot]
    return jnp.where(is_local, home_part * NB + block_lists, remote).astype(jnp.int32)

def smooth_step(field, edge_tiles, sources, degree):
    feat_width = field.shape[0]
    blocks = field.reshape(feat_width, -1, BLK).astype(jnp.float32)

    def single_block(inputs):
        tile_block, src_block, deg_block = inputs
        picked = blocks[:, src_block, :]
        return jnp.einsum('dks,kst->dt', picked, tile_block.astype(jnp.float32)) / deg_block[None]
    result = lax.map(single_block, (edge_tiles, sources, degree))
    return jnp.transpose(result, (1, 0, 2)).reshape(feat_width, -1).astype(jnp.bfloat16)

def reference(features, edge_tiles, block_lists, send_lists, train_ids, owners, cotangent, query_weight, key_weight, value_weight, out_weight, up_weight, down_weight):
    sources = global_sources(block_lists, send_lists)
    degree = lax.optimization_barrier(jnp.sum(edge_tiles.astype(jnp.float32), axis=(1, 2)))
    current = features
    hop_list = []
    for hop_index in range(HOPS):
        applied_once = smooth_step(current, edge_tiles, sources, degree)
        applied_twice = smooth_step(applied_once, edge_tiles, sources, degree)
        current = (0.5 * current.astype(jnp.float32) + applied_once.astype(jnp.float32) + applied_twice.astype(jnp.float32)).astype(jnp.bfloat16)
        hop_list.append(current)
    hop_tokens = jnp.stack(hop_list)
    everything = jnp.concatenate([features[None], hop_tokens], axis=0)
    part_of = jnp.arange(TRAINS, dtype=jnp.int32) // TRAIN_PART
    picked = everything[:, :, part_of * NODES_PART + train_ids]
    onehot = (owners[:, 0:1] == jnp.arange(DEVICES, dtype=jnp.int32)[None]).astype(jnp.float32)
    counts = lax.optimization_barrier(jnp.sum(onehot, axis=0))
    row_scale = lax.optimization_barrier(jnp.sum(onehot * (1.0 / counts)[None], axis=1))
    scaled = (cotangent.astype(jnp.float32) * row_scale[None, None]).astype(jnp.bfloat16)
    token_parts = picked.reshape(TOKS, D, PARTS_SIZE, TRAIN_PART).transpose(2, 0, 1, 3)
    grad_parts = scaled.reshape(TOKS, D, PARTS_SIZE, TRAIN_PART).transpose(2, 0, 1, 3)

    def accumulate(totals, inputs):
        part_terms = layer_grads(inputs[0], inputs[1], query_weight, key_weight, value_weight, out_weight, up_weight, down_weight)
        return (tuple((old_sum + new_term for old_sum, new_term in zip(totals, part_terms))), None)
    zero_sums = (jnp.zeros((4 * D, D), jnp.float32), jnp.zeros((FF, D), jnp.float32), jnp.zeros((FF, D), jnp.float32))
    totals, _ = lax.scan(accumulate, zero_sums, (token_parts, grad_parts))
    return (hop_tokens, totals[0], totals[1], totals[2])
```

```python
import functools
import math

import jax
import jax.numpy as jnp
from jax import lax
from jax.experimental import pallas as pl
from jax.experimental.pallas import tpu as pltpu
from jax.sharding import PartitionSpec as P

HEADS = 8
HOPS = 3
TOKS = 4
EPSILON = 1e-05
LANES = 128
MESH = pl.DeviceIdType.MESH
NT = (((1,), (1,)), ((), ()))
TN = (((0,), (0,)), ((), ()))
NN = (((1,), (0,)), ((), ()))
f32 = jnp.float32
bf16 = jnp.bfloat16


def dot(a, b, dims=NN):
    return lax.dot_general(a, b, dims, preferred_element_type=f32)


def hop_kernel(
    parts, lists, sends, feat, tiles_hbm, ids, cnt,
    hops_out, picked_out, cnt_out,
    pool_a, pool_b, fresh, tiles, degree, stage, onehot, cnt_buf,
    tile_sem, send_sem, recv_sem, cnt_send, cnt_recv,
):
    me = lax.axis_index("wide")
    blocks, fan = lists.shape
    slots = sends.shape[2]
    width = feat.shape[0]

    load = pltpu.make_async_copy(tiles_hbm, tiles, tile_sem)
    load.start()

    barrier = pltpu.get_barrier_semaphore()

    @pl.loop(1, parts)
    def _(d):
        peer = lax.rem(me + d, parts)
        pl.semaphore_signal(barrier, inc=1, device_id={"wide": peer}, device_id_type=MESH)

    for b in range(blocks):
        block = feat[:, b * LANES:(b + 1) * LANES]
        pool_a[b] = block
        fresh[b] = block
    pl.semaphore_wait(barrier, parts - 1)

    def halo_copy(pool, parity, dst, src):
        return pltpu.make_async_remote_copy(
            src_ref=stage.at[dst],
            dst_ref=pool.at[pl.ds(blocks + src * slots, slots)],
            send_sem=send_sem.at[dst],
            recv_sem=recv_sem.at[parity, src],
            device_id={"wide": dst},
            device_id_type=MESH,
        )

    def count_copy(dst, src):
        return pltpu.make_async_remote_copy(
            src_ref=cnt,
            dst_ref=cnt_buf.at[src],
            send_sem=cnt_send.at[dst],
            recv_sem=cnt_recv.at[src],
            device_id={"wide": dst},
            device_id_type=MESH,
        )

    def start_halo(pool, parity):
        @pl.loop(1, parts)
        def _(d):
            peer = lax.rem(me + d, parts)
            for q in range(slots):
                stage[peer, q] = fresh[sends[0, peer, q]]
            halo_copy(pool, parity, peer, me).start()

        for q in range(slots):
            pool[blocks + me * slots + q] = fresh[sends[0, me, q]]

    def finish_halo(pool, parity):
        @pl.loop(1, parts)
        def _(d):
            peer = lax.rem(me + d, parts)
            halo_copy(pool, parity, me, peer).wait_recv()

        @pl.loop(1, parts)
        def _(d):
            peer = lax.rem(me + d, parts)
            halo_copy(pool, parity, peer, me).wait_send()

    def apply(pool, b):
        left = jnp.concatenate([pool[lists[b, k]] for k in range(fan)], axis=1)
        summed = dot(left, tiles[b])
        return (summed / degree[pl.ds(b, 1), :]).astype(bf16)

    start_halo(pool_a, 0)

    @pl.loop(1, parts)
    def _(d):
        peer = lax.rem(me + d, parts)
        count_copy(peer, me).start()

    node_count = onehot.shape[0]
    step = node_count // blocks

    @pl.loop(0, blocks)
    def _(b):
        start = pl.multiple_of(b * step, step)
        rows = lax.broadcasted_iota(jnp.int32, (step, onehot.shape[1]), 0) + start
        onehot[pl.ds(start, step), :] = jnp.where(rows == ids[...], 1.0, 0.0).astype(bf16)

    picked_out[0] = dot(feat[...], onehot[...]).astype(bf16)
    load.wait()

    @pl.loop(0, blocks)
    def _(b):
        degree[pl.ds(b, 1), :] = jnp.sum(tiles[b].astype(f32), axis=0, keepdims=True)

    @pl.loop(0, HOPS)
    def _(hop):
        finish_halo(pool_a, 0)

        @pl.loop(0, blocks, step=2)
        def _(b):
            for c in range(2):
                once = apply(pool_a, b + c)
                pool_b[b + c] = once
                fresh[b + c] = once

        start_halo(pool_b, 1)
        finish_halo(pool_b, 1)

        @pl.loop(0, blocks, step=2)
        def _(b):
            for c in range(2):
                twice = apply(pool_b, b + c).astype(f32)
                smooth = 0.5 * pool_a[b + c].astype(f32) + pool_b[b + c].astype(f32) + twice
                smooth = smooth.astype(bf16)
                pool_a[b + c] = smooth
                fresh[b + c] = smooth
                start = pl.multiple_of((b + c) * LANES, LANES)
                hops_out[hop, :, pl.ds(start, LANES)] = smooth

        @pl.when(hop < HOPS - 1)
        def _():
            start_halo(pool_a, 0)

        picked_out[hop + 1] = dot(hops_out[hop], onehot[...]).astype(bf16)

    cnt_buf[me] = cnt[...]

    @pl.loop(1, parts)
    def _(d):
        peer = lax.rem(me + d, parts)
        count_copy(me, peer).wait_recv()

    @pl.loop(1, parts)
    def _(d):
        peer = lax.rem(me + d, parts)
        count_copy(peer, me).wait_send()

    cnt_out[...] = jnp.sum(cnt_buf[...], axis=0)


def smooth_hops(features, edge_tiles, block_lists, send_lists, train_ids, counts):
    width, nodes = features.shape
    blocks, fan, size, _ = edge_tiles.shape
    parts, slots = send_lists.shape[1:]
    rows = train_ids.shape[0]
    halo = parts * slots
    vmem = pl.BlockSpec(memory_space=pltpu.VMEM)
    smem = pl.BlockSpec(memory_space=pltpu.SMEM)
    return pl.pallas_call(
        functools.partial(hop_kernel, parts),
        out_shape=(
            jax.ShapeDtypeStruct((HOPS, width, nodes), bf16),
            jax.ShapeDtypeStruct((TOKS, width, rows), bf16),
            jax.ShapeDtypeStruct(counts.shape, f32),
        ),
        in_specs=[smem, smem, vmem, pl.BlockSpec(memory_space=pl.ANY), vmem, vmem],
        out_specs=(vmem, vmem, vmem),
        scratch_shapes=[
            pltpu.VMEM((blocks + halo, width, size), bf16),
            pltpu.VMEM((blocks + halo, width, size), bf16),
            pltpu.VMEM((blocks, width, size), bf16),
            pltpu.VMEM((blocks, fan * size, size), bf16),
            pltpu.VMEM((blocks, size), f32),
            pltpu.VMEM((parts, slots, width, size), bf16),
            pltpu.VMEM((nodes, rows), bf16),
            pltpu.VMEM((parts,) + counts.shape, f32),
            pltpu.SemaphoreType.DMA,
            pltpu.SemaphoreType.DMA((parts,)),
            pltpu.SemaphoreType.DMA((2, parts)),
            pltpu.SemaphoreType.DMA((parts,)),
            pltpu.SemaphoreType.DMA((parts,)),
        ],
        compiler_params=pltpu.CompilerParams(
            collective_id=0, has_side_effects=True, vmem_limit_bytes=56 * 2**20
        ),
        name="smooth_hops",
    )(
        block_lists, send_lists, features,
        edge_tiles.reshape(blocks, fan * size, size),
        train_ids.reshape(1, rows), counts,
    )


def normalize(hidden):
    center = hidden - jnp.mean(hidden, axis=0, keepdims=True)
    inverse = lax.rsqrt(jnp.mean(center * center, axis=0, keepdims=True) + EPSILON)
    return center * inverse, inverse


def layer_kernel(
    packed, wq, wk, wv, wo, wu, wd, attn_out, up_out, down_out, nb_ref, cot_ref, g_ref
):
    share = packed.shape[2]
    width = packed.shape[1]
    cols = TOKS * share
    head = width // HEADS
    scale = 1.0 / math.sqrt(head)
    x = jnp.concatenate([packed[t].astype(f32) for t in range(TOKS)], axis=1)
    cot32 = jnp.concatenate([packed[TOKS + t].astype(f32) for t in range(TOKS)], axis=1)
    cot_ref[...] = cot32.astype(bf16)

    def ahead(v, j):
        return v if j == 0 else pltpu.roll(v, cols - j * share, 1)

    def back(v, j):
        return v if j == 0 else pltpu.roll(v, j * share, 1)

    def head_sum(v):
        return jnp.sum(v.reshape(HEADS, head, cols), axis=1)

    def spread(v):
        return jnp.broadcast_to(v[:, None, :], (HEADS, head, cols)).reshape(width, cols)

    def low(v):
        return v.astype(bf16).astype(f32)

    normed_a = normalize(x)[0].astype(bf16)
    query = low(dot(wq[...], normed_a))
    key = low(dot(wk[...], normed_a))
    value = low(dot(wv[...], normed_a))
    scores = [head_sum(query * ahead(key, j)) * scale for j in range(TOKS)]
    top = functools.reduce(jnp.maximum, scores)
    exps = [jnp.exp(s - top) for s in scores]
    total = functools.reduce(jnp.add, exps)
    probs = [e / total for e in exps]
    probs_low = [low(p) for p in probs]
    mixed = functools.reduce(
        jnp.add, [spread(probs_low[j]) * ahead(value, j) for j in range(TOKS)]
    ).astype(bf16)
    residual = low(x + dot(wo[...], mixed))
    second, inverse = normalize(residual)
    nb_ref[...] = second.astype(bf16)
    g_ref[...] = jnp.zeros_like(g_ref)
    chunk = 256
    slope = math.sqrt(2.0 / math.pi)

    @pl.loop(0, wu.shape[0] // chunk)
    def _(i):
        rows = pl.ds(pl.multiple_of(i * chunk, chunk), chunk)
        up = wu[rows, :]
        cot = cot_ref[...]
        normed_b = nb_ref[...]
        pre = dot(up, normed_b)
        square = pre * pre
        tanh = jnp.tanh(slope * (pre + 0.044715 * (square * pre)))
        activated = (0.5 * pre * (1.0 + tanh)).astype(bf16)
        deriv = 0.5 * (1.0 + tanh) + 0.5 * pre * (1.0 - tanh * tanh) * (
            slope * (1.0 + 3.0 * 0.044715 * square)
        )
        down_out[rows, :] = dot(activated, cot, NT).astype(bf16)
        grad_pre = (dot(wd[rows, :], cot) * deriv).astype(bf16)
        up_out[rows, :] = dot(grad_pre, normed_b, NT).astype(bf16)
        g_ref[...] += dot(up, grad_pre, TN)

    upstream = g_ref[...]
    grad_resid = (
        cot32
        + inverse
        * (
            upstream
            - jnp.mean(upstream, axis=0, keepdims=True)
            - second * jnp.mean(upstream * second, axis=0, keepdims=True)
        )
    ).astype(bf16)
    attn_out[3 * width:4 * width, :] = dot(grad_resid, mixed, NT).astype(bf16)
    grad_mixed = low(dot(wo[...], grad_resid, TN))
    grad_probs = [head_sum(grad_mixed * ahead(value, j)) for j in range(TOKS)]
    grad_value = functools.reduce(
        jnp.add, [back(spread(probs_low[j]) * grad_mixed, j) for j in range(TOKS)]
    ).astype(bf16)
    attn_out[2 * width:3 * width, :] = dot(grad_value, normed_a, NT).astype(bf16)
    inner = functools.reduce(jnp.add, [p * g for p, g in zip(probs, grad_probs)])
    grad_scores = [low(p * (g - inner) * scale) for p, g in zip(probs, grad_probs)]
    grad_query = functools.reduce(
        jnp.add, [spread(grad_scores[j]) * ahead(key, j) for j in range(TOKS)]
    ).astype(bf16)
    attn_out[0:width, :] = dot(grad_query, normed_a, NT).astype(bf16)
    grad_key = functools.reduce(
        jnp.add, [back(spread(grad_scores[j]) * query, j) for j in range(TOKS)]
    ).astype(bf16)
    attn_out[width:2 * width, :] = dot(grad_key, normed_a, NT).astype(bf16)


def layer_sums(packed, wq, wk, wv, wo, wu, wd):
    width = packed.shape[1]
    cols = TOKS * packed.shape[2]
    vmem = pl.BlockSpec(memory_space=pltpu.VMEM)
    return pl.pallas_call(
        layer_kernel,
        out_shape=(
            jax.ShapeDtypeStruct((4 * width, width), bf16),
            jax.ShapeDtypeStruct(wu.shape, bf16),
            jax.ShapeDtypeStruct(wd.shape, bf16),
        ),
        in_specs=[vmem] * 7,
        out_specs=(vmem, vmem, vmem),
        scratch_shapes=[
            pltpu.VMEM((width, cols), bf16),
            pltpu.VMEM((width, cols), bf16),
            pltpu.VMEM((width, cols), f32),
        ],
        compiler_params=pltpu.CompilerParams(vmem_limit_bytes=48 * 2**20),
        name="layer_sums",
    )(packed, wq, wk, wv, wo, wu, wd)


def halving_sum(term, bits, order):
    count = len(bits)
    depth = term.shape[1]
    term = term.reshape((2,) * count + (-1, depth))
    left = list(range(count))
    for place, bit in enumerate(order):
        axis, shift = bits[bit]
        size = lax.axis_size(axis)
        mine = lax.rem(lax.axis_index(axis) // (1 << shift), 2)
        dim = left.index(bit)
        left.remove(bit)
        sent = lax.dynamic_index_in_dim(term, 1 - mine, dim, keepdims=False)
        kept = lax.dynamic_index_in_dim(term, mine, dim, keepdims=False)
        got = lax.ppermute(sent, axis, [(i, i ^ (1 << shift)) for i in range(size)])
        term = kept.astype(f32) + got.astype(f32)
        if place < count - 1:
            term = term.astype(bf16)
    return term


def on_device(
    features, edge_tiles, block_lists, send_lists, train_ids, owners, cotangent,
    query_weight, key_weight, value_weight, out_weight, up_weight, down_weight,
):
    parts = lax.axis_size("wide")
    narrow = lax.axis_size("narrow")
    devices = parts * narrow
    rows = train_ids.shape[0]
    share = rows // narrow
    width = features.shape[0]
    padded = -(-devices // LANES) * LANES
    onehot = (owners == jnp.arange(padded, dtype=jnp.int32)[None]).astype(f32)
    own_counts = jnp.broadcast_to(jnp.sum(onehot, axis=0)[None], (8, padded))
    hop_tokens, picked, counts = smooth_hops(
        features, edge_tiles, block_lists, send_lists, train_ids, own_counts
    )
    inverse = 1.0 / jnp.maximum(counts[0], 1.0)
    row_scale = jnp.sum(onehot * inverse[None], axis=1)
    scaled = (cotangent.astype(f32) * row_scale[None, None]).astype(bf16)
    packed = jnp.concatenate([picked, scaled], axis=0).reshape(2 * TOKS, width, narrow, share)
    packed = lax.all_to_all(packed, "narrow", split_axis=2, concat_axis=1, tiled=True)
    packed = packed.reshape(2 * TOKS, width * narrow, share)
    attn_part, up_part, down_part = layer_sums(
        packed, query_weight, key_weight, value_weight, out_weight, up_weight, down_weight
    )
    bits = [("wide", s) for s in reversed(range(parts.bit_length() - 1))]
    wide_bits = list(range(len(bits)))
    bits += [("narrow", s) for s in reversed(range(narrow.bit_length() - 1))]
    narrow_bits = list(range(len(wide_bits), len(bits)))
    core, across = narrow_bits[-1], narrow_bits[:-1][::-1]
    low_wide, high_wide = wide_bits[-1:], wide_bits[:-1][::-1]
    orders = (
        [core] + across + low_wide + high_wide,
        [core] + low_wide + high_wide + across,
        [core] + high_wide + across + low_wide,
    )
    return (
        hop_tokens,
        halving_sum(attn_part, bits, orders[0]),
        halving_sum(up_part, bits, orders[1]),
        halving_sum(down_part, bits, orders[2]),
    )


def solution(mesh):
    in_specs = (
        P("narrow", "wide"),
        P("wide", None, None, None),
        P("wide", None),
        P("wide", None, None),
        P("wide"),
        P("wide", None),
        P(None, "narrow", "wide"),
        P(),
        P(),
        P(),
        P(),
        P(),
        P(),
    )
    out_specs = (
        P(None, "narrow", "wide"),
        P(("wide", "narrow"), None),
        P(("wide", "narrow"), None),
        P(("wide", "narrow"), None),
    )
    return jax.shard_map(
        on_device, mesh=mesh, in_specs=in_specs, out_specs=out_specs, check_vma=False
    )
```

```python
import functools
import math

import jax
import jax.numpy as jnp
from jax import lax
from jax.experimental import pallas as pl
from jax.experimental.pallas import tpu as pltpu
from jax.sharding import PartitionSpec as P

HEADS = 8
HOPS = 3
TOKS = 4
EPSILON = 1e-05
LANES = 128
MESH = pl.DeviceIdType.MESH
NT = (((1,), (1,)), ((), ()))
TN = (((0,), (0,)), ((), ()))
NN = (((1,), (0,)), ((), ()))
f32 = jnp.float32
bf16 = jnp.bfloat16


def dot(a, b, dims=NN):
    return lax.dot_general(a, b, dims, preferred_element_type=f32)


def hop_kernel(
    parts, narrow, lists, sends, feat, tiles_hbm, ids, owners, cot,
    hops_out, packed_out,
    a_first, a_second, b_first, b_second, fresh_first, fresh_second,
    stage_first, stage_second, tiles, degree, onehot, cnt, cnt_buf, picked, cut, land,
    tile_sem, send_sem, recv_sem, cnt_send, cnt_recv, cut_send, cut_recv,
):
    me = lax.axis_index("wide")
    mine = lax.axis_index("narrow")
    blocks, fan = lists.shape
    slots = sends.shape[2]
    width = feat.shape[0]
    half = width // 2
    rows = ids.shape[1]
    share = rows // narrow
    pool_a = (a_first, a_second)
    pool_b = (b_first, b_second)
    fresh = (fresh_first, fresh_second)
    stage = (stage_first, stage_second)

    load = pltpu.make_async_copy(tiles_hbm, tiles, tile_sem)
    load.start()

    barrier = pltpu.get_barrier_semaphore()

    @pl.loop(1, parts)
    def _(d):
        peer = lax.rem(me + d, parts)
        pl.semaphore_signal(barrier, inc=1, device_id={"wide": peer}, device_id_type=MESH)

    @pl.loop(1, narrow)
    def _(d):
        peer = lax.rem(mine + d, narrow)
        pl.semaphore_signal(barrier, inc=1, device_id={"narrow": peer}, device_id_type=MESH)

    for h in range(2):
        for b in range(blocks):
            block = feat[h * half:(h + 1) * half, b * LANES:(b + 1) * LANES]
            pool_a[h][b] = block
            fresh[h][b] = block
    named = lax.broadcasted_iota(jnp.int32, (cnt.shape[0], rows), 0) == owners[...]
    named = jnp.where(named, 1.0, 0.0)
    cnt[...] = jnp.broadcast_to(jnp.sum(named, axis=1, keepdims=True), cnt.shape)
    pl.semaphore_wait(barrier, parts + narrow - 2)

    def halo_copy(pools, parity, h, dst, src):
        return pltpu.make_async_remote_copy(
            src_ref=stage[h].at[dst],
            dst_ref=pools[h].at[pl.ds(blocks + src * slots, slots)],
            send_sem=send_sem.at[h, dst],
            recv_sem=recv_sem.at[2 * parity + h, src],
            device_id={"wide": dst},
            device_id_type=MESH,
        )

    def count_copy(dst, src):
        return pltpu.make_async_remote_copy(
            src_ref=cnt,
            dst_ref=cnt_buf.at[src],
            send_sem=cnt_send.at[dst],
            recv_sem=cnt_recv.at[src],
            device_id={"wide": dst},
            device_id_type=MESH,
        )

    def cut_copy(piece, dst, src):
        return pltpu.make_async_remote_copy(
            src_ref=cut.at[piece, dst],
            dst_ref=land.at[piece, pl.ds(src * width, width)],
            send_sem=cut_send.at[piece, dst],
            recv_sem=cut_recv.at[piece, src],
            device_id={"narrow": dst},
            device_id_type=MESH,
        )

    def start_halo(pools, parity, h):
        @pl.loop(1, parts)
        def _(d):
            peer = lax.rem(me + d, parts)
            for q in range(slots):
                stage[h][peer, q] = fresh[h][sends[0, peer, q]]
            halo_copy(pools, parity, h, peer, me).start()

        for q in range(slots):
            pools[h][blocks + me * slots + q] = fresh[h][sends[0, me, q]]

    def finish_halo(pools, parity, h):
        @pl.loop(1, parts)
        def _(d):
            peer = lax.rem(me + d, parts)
            halo_copy(pools, parity, h, me, peer).wait_recv()

        @pl.loop(1, parts)
        def _(d):
            peer = lax.rem(me + d, parts)
            halo_copy(pools, parity, h, peer, me).wait_send()

    def start_cut(piece, one, two):
        for n in range(narrow):
            span = slice(n * share, (n + 1) * share)
            cut[piece, n] = jnp.concatenate([one[:, span], two[:, span]], axis=1).astype(bf16)

        @pl.loop(1, narrow)
        def _(d):
            peer = lax.rem(mine + d, narrow)
            cut_copy(piece, peer, mine).start()

        land[piece, pl.ds(mine * width, width), :] = cut[piece, mine]

    def apply(pool, b):
        left = jnp.concatenate([pool[lists[b, k]] for k in range(fan)], axis=1)
        summed = dot(left, tiles[b])
        return (summed / degree[pl.ds(b, 1), :]).astype(bf16)

    for h in range(2):
        start_halo(pool_a, 0, h)

    @pl.loop(1, parts)
    def _(d):
        peer = lax.rem(me + d, parts)
        count_copy(peer, me).start()

    step = onehot.shape[0] // blocks

    @pl.loop(0, blocks)
    def _(b):
        start = pl.multiple_of(b * step, step)
        node = lax.broadcasted_iota(jnp.int32, (step, rows), 0) + start
        onehot[pl.ds(start, step), :] = jnp.where(node == ids[...], 1.0, 0.0).astype(bf16)

    picked[0] = dot(feat[...], onehot[...])
    load.wait()

    @pl.loop(0, blocks)
    def _(b):
        degree[pl.ds(b, 1), :] = jnp.sum(tiles[b].astype(f32), axis=0, keepdims=True)

    cnt_buf[me] = cnt[...]

    @pl.loop(1, parts)
    def _(d):
        peer = lax.rem(me + d, parts)
        count_copy(me, peer).wait_recv()

    counts = jnp.sum(cnt_buf[...], axis=0)[:, 0:1]
    scale = jnp.sum(named * (1.0 / jnp.maximum(counts, 1.0)), axis=0, keepdims=True)
    for pair in range(2):
        start_cut(
            pair,
            cot[2 * pair].astype(f32) * scale,
            cot[2 * pair + 1].astype(f32) * scale,
        )

    unroll = 4

    @pl.loop(0, HOPS)
    def _(hop):
        for h in range(2):
            finish_halo(pool_a, 0, h)

            @pl.loop(0, blocks, step=unroll)
            def _(b):
                for c in range(unroll):
                    once = apply(pool_a[h], b + c)
                    pool_b[h][b + c] = once
                    fresh[h][b + c] = once

            start_halo(pool_b, 1, h)

        for h in range(2):
            finish_halo(pool_b, 1, h)

            @pl.loop(0, blocks, step=unroll)
            def _(b):
                for c in range(unroll):
                    twice = apply(pool_b[h], b + c).astype(f32)
                    smooth = 0.5 * pool_a[h][b + c].astype(f32) + pool_b[h][b + c].astype(f32)
                    smooth = (smooth + twice).astype(bf16)
                    pool_a[h][b + c] = smooth
                    fresh[h][b + c] = smooth
                    start = pl.multiple_of((b + c) * LANES, LANES)
                    hops_out[hop, h * half:(h + 1) * half, pl.ds(start, LANES)] = smooth

            @pl.when(hop < HOPS - 1)
            def _():
                start_halo(pool_a, 0, h)

        picked[hop + 1] = dot(hops_out[hop], onehot[...])

        @pl.when(hop == 0)
        def _():
            start_cut(2, picked[0], picked[1])

    start_cut(3, picked[2], picked[3])

    @pl.loop(1, parts)
    def _(d):
        peer = lax.rem(me + d, parts)
        count_copy(peer, me).wait_send()

    for piece in range(TOKS):
        @pl.loop(1, narrow)
        def _(d):
            peer = lax.rem(mine + d, narrow)
            cut_copy(piece, mine, peer).wait_recv()
            cut_copy(piece, peer, mine).wait_send()

    packed_out[...] = land[...]


def smooth_hops(
    parts, narrow, features, edge_tiles, block_lists, send_lists, train_ids, owners, cotangent
):
    width, nodes = features.shape
    blocks, fan, size, _ = edge_tiles.shape
    slots = send_lists.shape[2]
    rows = train_ids.shape[0]
    pool = blocks + parts * slots
    half = width // 2
    devices = -(-parts * narrow // 8) * 8
    lanes = 2 * rows // narrow
    vmem = pl.BlockSpec(memory_space=pltpu.VMEM)
    smem = pl.BlockSpec(memory_space=pltpu.SMEM)
    return pl.pallas_call(
        functools.partial(hop_kernel, parts, narrow),
        out_shape=(
            jax.ShapeDtypeStruct((HOPS, width, nodes), bf16),
            jax.ShapeDtypeStruct((TOKS, width * narrow, lanes), bf16),
        ),
        in_specs=[smem, smem, vmem, pl.BlockSpec(memory_space=pl.ANY), vmem, vmem, vmem],
        out_specs=(vmem, vmem),
        scratch_shapes=[pltpu.VMEM((pool, half, size), bf16)] * 4
        + [pltpu.VMEM((blocks, half, size), bf16)] * 2
        + [pltpu.VMEM((parts, slots, half, size), bf16)] * 2
        + [
            pltpu.VMEM((blocks, fan * size, size), bf16),
            pltpu.VMEM((blocks, size), f32),
            pltpu.VMEM((nodes, rows), bf16),
            pltpu.VMEM((devices, LANES), f32),
            pltpu.VMEM((parts, devices, LANES), f32),
            pltpu.VMEM((TOKS, width, rows), f32),
            pltpu.VMEM((TOKS, narrow, width, lanes), bf16),
            pltpu.VMEM((TOKS, width * narrow, lanes), bf16),
            pltpu.SemaphoreType.DMA,
            pltpu.SemaphoreType.DMA((2, parts)),
            pltpu.SemaphoreType.DMA((4, parts)),
            pltpu.SemaphoreType.DMA((parts,)),
            pltpu.SemaphoreType.DMA((parts,)),
            pltpu.SemaphoreType.DMA((TOKS, narrow)),
            pltpu.SemaphoreType.DMA((TOKS, narrow)),
        ],
        compiler_params=pltpu.CompilerParams(
            collective_id=0, has_side_effects=True, vmem_limit_bytes=56 * 2**20
        ),
        name="smooth_hops",
    )(
        block_lists, send_lists, features,
        edge_tiles.reshape(blocks, fan * size, size),
        train_ids.reshape(1, rows), owners.reshape(1, rows), cotangent,
    )


def normalize(hidden):
    center = hidden - jnp.mean(hidden, axis=0, keepdims=True)
    inverse = lax.rsqrt(jnp.mean(center * center, axis=0, keepdims=True) + EPSILON)
    return center * inverse, inverse


def layer_kernel(
    bits, orders, packed, wq, wk, wv, wo, wu, wd, attn_out, up_out, down_out,
    nb_ref, cot_ref, g_ref, attn_sum, up_sum, down_sum, attn_in, up_in, down_in,
    send_sem, recv_sem,
):
    outs = (attn_out, up_out, down_out)
    terms = (attn_sum, up_sum, down_sum)
    incoming = (attn_in, up_in, down_in)
    devices, piece = attn_sum.shape[:2]
    stages = len(bits)
    me = [lax.axis_index(axis) for axis, _, _ in bits]
    own = [lax.rem(lax.div(i, 1 << shift), 2) for i, (_, shift, _) in zip(me, bits)]
    partner = [
        {axis: i + (1 - 2 * m) * (1 << shift)} for i, m, (axis, shift, _) in zip(me, own, bits)
    ]
    barrier = pltpu.get_barrier_semaphore()
    for peer in partner:
        pl.semaphore_signal(barrier, inc=1, device_id=peer, device_id_type=MESH)
    pl.semaphore_wait(barrier, stages)

    def place(chain, block):
        spot = 0
        for bit in orders[chain]:
            weight = bits[bit][2]
            if isinstance(block, int):
                spot = 2 * spot + block // weight % 2
            else:
                spot = 2 * spot + lax.rem(lax.div(block, weight), 2)
        return spot

    def put(chain, first, value):
        value = value.astype(bf16)
        for c in range(value.shape[0] // piece):
            terms[chain][place(chain, first + c)] = value[c * piece:(c + 1) * piece, :]

    bases = [[0], [0], [0]]

    def exchange(chain, stage):
        bit = orders[chain][stage]
        half = devices >> (stage + 1)
        base = bases[chain][stage]
        if len(bases[chain]) == stage + 1:
            bases[chain].append(base + own[bit] * half)
        return pltpu.make_async_remote_copy(
            src_ref=terms[chain].at[pl.ds(base + (1 - own[bit]) * half, half)],
            dst_ref=incoming[chain].at[pl.ds(devices - 2 * half, half)],
            send_sem=send_sem.at[chain, stage],
            recv_sem=recv_sem.at[chain, stage],
            device_id=partner[bit],
            device_id_type=MESH,
        )

    def absorb(chain, stage):
        exchange(chain, stage).wait_recv()
        half = devices >> (stage + 1)
        base = bases[chain][stage + 1]

        if stage == stages - 1:
            outs[chain][...] = (
                terms[chain][base].astype(f32) + incoming[chain][devices - 2].astype(f32)
            )
        else:
            @pl.loop(0, half)
            def _(i):
                total = terms[chain][base + i].astype(f32)
                total = total + incoming[chain][devices - 2 * half + i].astype(f32)
                terms[chain][base + i] = total.astype(bf16)

            exchange(chain, stage + 1).start()

    share = packed.shape[2] // 2
    width = packed.shape[1]
    cols = TOKS * share
    head = width // HEADS
    scale = 1.0 / math.sqrt(head)
    cot32 = jnp.concatenate([packed[t].astype(f32) for t in range(2)], axis=1)
    x = jnp.concatenate([packed[2 + t].astype(f32) for t in range(2)], axis=1)
    cot_ref[...] = cot32.astype(bf16)

    def ahead(v, j):
        return v if j == 0 else pltpu.roll(v, cols - j * share, 1)

    def back(v, j):
        return v if j == 0 else pltpu.roll(v, j * share, 1)

    def head_sum(v):
        return jnp.sum(v.reshape(HEADS, head, cols), axis=1)

    def spread(v):
        return jnp.broadcast_to(v[:, None, :], (HEADS, head, cols)).reshape(width, cols)

    def low(v):
        return v.astype(bf16).astype(f32)

    normed_a = normalize(x)[0].astype(bf16)
    query = low(dot(wq[...], normed_a))
    key = low(dot(wk[...], normed_a))
    value = low(dot(wv[...], normed_a))
    scores = [head_sum(query * ahead(key, j)) * scale for j in range(TOKS)]
    top = functools.reduce(jnp.maximum, scores)
    exps = [jnp.exp(s - top) for s in scores]
    total = functools.reduce(jnp.add, exps)
    probs = [e / total for e in exps]
    probs_low = [low(p) for p in probs]
    mixed = functools.reduce(
        jnp.add, [spread(probs_low[j]) * ahead(value, j) for j in range(TOKS)]
    ).astype(bf16)
    residual = low(x + dot(wo[...], mixed))
    second, inverse = normalize(residual)
    nb_ref[...] = second.astype(bf16)
    g_ref[...] = jnp.zeros_like(g_ref)
    chunk = 256
    slope = math.sqrt(2.0 / math.pi)

    @pl.loop(0, wu.shape[0] // chunk)
    def _(i):
        rows = pl.ds(pl.multiple_of(i * chunk, chunk), chunk)
        up = wu[rows, :]
        cot = cot_ref[...]
        normed_b = nb_ref[...]
        pre = dot(up, normed_b)
        square = pre * pre
        tanh = jnp.tanh(slope * (pre + 0.044715 * (square * pre)))
        activated = (0.5 * pre * (1.0 + tanh)).astype(bf16)
        deriv = 0.5 * (1.0 + tanh) + 0.5 * pre * (1.0 - tanh * tanh) * (
            slope * (1.0 + 3.0 * 0.044715 * square)
        )
        put(2, i * (chunk // piece), dot(activated, cot, NT))
        grad_pre = (dot(wd[rows, :], cot) * deriv).astype(bf16)
        put(1, i * (chunk // piece), dot(grad_pre, normed_b, NT))
        g_ref[...] += dot(up, grad_pre, TN)

    exchange(2, 0).start()
    exchange(1, 0).start()
    group = width // piece
    upstream = g_ref[...]
    grad_resid = (
        cot32
        + inverse
        * (
            upstream
            - jnp.mean(upstream, axis=0, keepdims=True)
            - second * jnp.mean(upstream * second, axis=0, keepdims=True)
        )
    ).astype(bf16)
    put(0, 3 * group, dot(grad_resid, mixed, NT))
    grad_mixed = low(dot(wo[...], grad_resid, TN))
    grad_probs = [head_sum(grad_mixed * ahead(value, j)) for j in range(TOKS)]
    grad_value = functools.reduce(
        jnp.add, [back(spread(probs_low[j]) * grad_mixed, j) for j in range(TOKS)]
    ).astype(bf16)
    put(0, 2 * group, dot(grad_value, normed_a, NT))
    inner = functools.reduce(jnp.add, [p * g for p, g in zip(probs, grad_probs)])
    grad_scores = [low(p * (g - inner) * scale) for p, g in zip(probs, grad_probs)]
    grad_query = functools.reduce(
        jnp.add, [spread(grad_scores[j]) * ahead(key, j) for j in range(TOKS)]
    ).astype(bf16)
    put(0, 0, dot(grad_query, normed_a, NT))
    grad_key = functools.reduce(
        jnp.add, [back(spread(grad_scores[j]) * query, j) for j in range(TOKS)]
    ).astype(bf16)
    put(0, group, dot(grad_key, normed_a, NT))
    exchange(0, 0).start()
    for stage in range(stages):
        for chain in (2, 1, 0):
            absorb(chain, stage)
    for chain in range(3):
        for stage in range(stages):
            exchange(chain, stage).wait_send()


def layer_sums(parts, narrow, packed, wq, wk, wv, wo, wu, wd):
    width = packed.shape[1]
    cols = 2 * packed.shape[2]
    devices = parts * narrow
    piece = wu.shape[0] // devices
    bits = [("narrow", s, 1 << s) for s in range(narrow.bit_length() - 1)]
    bits += [("wide", s, narrow << s) for s in range(parts.bit_length() - 1)]
    core, low = 0, narrow.bit_length() - 1
    across = list(range(1, low))
    high = list(range(low + 1, len(bits)))
    orders = (
        [core] + across + [low] + high,
        [core, low] + high + across,
        [core] + high + across + [low],
    )
    vmem = pl.BlockSpec(memory_space=pltpu.VMEM)
    return pl.pallas_call(
        functools.partial(layer_kernel, bits, orders),
        out_shape=(jax.ShapeDtypeStruct((piece, width), f32),) * 3,
        in_specs=[vmem] * 7,
        out_specs=(vmem, vmem, vmem),
        scratch_shapes=[
            pltpu.VMEM((width, cols), bf16),
            pltpu.VMEM((width, cols), bf16),
            pltpu.VMEM((width, cols), f32),
        ]
        + [pltpu.VMEM((devices, piece, width), bf16)] * 6
        + [pltpu.SemaphoreType.DMA((3, len(bits)))] * 2,
        compiler_params=pltpu.CompilerParams(
            collective_id=1, has_side_effects=True, vmem_limit_bytes=48 * 2**20
        ),
        name="layer_sums",
    )(packed, wq, wk, wv, wo, wu, wd)


def on_device(
    features, edge_tiles, block_lists, send_lists, train_ids, owners, cotangent,
    query_weight, key_weight, value_weight, out_weight, up_weight, down_weight,
):
    parts = lax.axis_size("wide")
    narrow = lax.axis_size("narrow")
    hop_tokens, packed = smooth_hops(
        parts, narrow, features, edge_tiles, block_lists, send_lists, train_ids, owners, cotangent
    )
    sums = layer_sums(
        parts, narrow, packed,
        query_weight, key_weight, value_weight, out_weight, up_weight, down_weight,
    )
    return (hop_tokens, *sums)


def solution(mesh):
    in_specs = (
        P("narrow", "wide"),
        P("wide", None, None, None),
        P("wide", None),
        P("wide", None, None),
        P("wide"),
        P("wide", None),
        P(None, "narrow", "wide"),
        P(),
        P(),
        P(),
        P(),
        P(),
        P(),
    )
    out_specs = (
        P(None, "narrow", "wide"),
        P(("wide", "narrow"), None),
        P(("wide", "narrow"), None),
        P(("wide", "narrow"), None),
    )
    return jax.shard_map(
        on_device, mesh=mesh, in_specs=in_specs, out_specs=out_specs, check_vma=False
    )
```

```python
import functools
import math

import jax
import jax.numpy as jnp
from jax import lax
from jax.experimental import pallas as pl
from jax.experimental.pallas import tpu as pltpu
from jax.sharding import PartitionSpec as P

HEADS = 8
HOPS = 3
TOKS = 4
EPSILON = 1e-05
LANES = 128
MESH = pl.DeviceIdType.MESH
NT = (((1,), (1,)), ((), ()))
TN = (((0,), (0,)), ((), ()))
NN = (((1,), (0,)), ((), ()))
f32 = jnp.float32
bf16 = jnp.bfloat16


def dot(a, b, dims=NN):
    return lax.dot_general(a, b, dims, preferred_element_type=f32)


def hop_kernel(
    parts, narrow, lists, sends, feat, tiles_hbm, ids, owners, cot,
    hops_out, packed_out,
    a_first, a_second, b_first, b_second, fresh_first, fresh_second,
    stage_first, stage_second, tiles, degree, onehot, cnt, cnt_buf, picked, cut, land,
    tile_sem, send_sem, recv_sem, cnt_send, cnt_recv, cut_send, cut_recv,
):
    me = lax.axis_index("wide")
    mine = lax.axis_index("narrow")
    fan, blocks = lists.shape
    slots = sends.shape[1]
    width = feat.shape[0]
    half = width // 2
    rows = ids.shape[1]
    share = rows // narrow
    pool_a = (a_first, a_second)
    pool_b = (b_first, b_second)
    fresh = (fresh_first, fresh_second)
    stage = (stage_first, stage_second)

    load = pltpu.make_async_copy(tiles_hbm, tiles, tile_sem)
    load.start()

    barrier = pltpu.get_barrier_semaphore()

    @pl.loop(1, parts)
    def _(d):
        peer = lax.rem(me + d, parts)
        pl.semaphore_signal(barrier, inc=1, device_id={"wide": peer}, device_id_type=MESH)

    @pl.loop(1, narrow)
    def _(d):
        peer = lax.rem(mine + d, narrow)
        pl.semaphore_signal(barrier, inc=1, device_id={"narrow": peer}, device_id_type=MESH)

    for h in range(2):
        for b in range(blocks):
            block = feat[h * half:(h + 1) * half, b * LANES:(b + 1) * LANES]
            pool_a[h][b] = block
            fresh[h][b] = block
    named = lax.broadcasted_iota(jnp.int32, (cnt.shape[0], rows), 0) == owners[...]
    named = jnp.where(named, 1.0, 0.0)
    cnt[...] = jnp.broadcast_to(jnp.sum(named, axis=1, keepdims=True), cnt.shape)
    pl.semaphore_wait(barrier, parts + narrow - 2)

    def halo_copy(pools, parity, h, dst, src):
        return pltpu.make_async_remote_copy(
            src_ref=stage[h].at[dst],
            dst_ref=pools[h].at[pl.ds(blocks + src * slots, slots)],
            send_sem=send_sem.at[h, dst],
            recv_sem=recv_sem.at[2 * parity + h, src],
            device_id={"wide": dst},
            device_id_type=MESH,
        )

    def count_copy(dst, src):
        return pltpu.make_async_remote_copy(
            src_ref=cnt,
            dst_ref=cnt_buf.at[src],
            send_sem=cnt_send.at[dst],
            recv_sem=cnt_recv.at[src],
            device_id={"wide": dst},
            device_id_type=MESH,
        )

    def cut_copy(piece, dst, src):
        return pltpu.make_async_remote_copy(
            src_ref=cut.at[piece, dst],
            dst_ref=land.at[piece, pl.ds(src * width, width)],
            send_sem=cut_send.at[piece, dst],
            recv_sem=cut_recv.at[piece, src],
            device_id={"narrow": dst},
            device_id_type=MESH,
        )

    def start_halo(pools, parity, h):
        @pl.loop(1, parts)
        def _(d):
            peer = lax.rem(me + d, parts)
            for q in range(slots):
                stage[h][peer, q] = fresh[h][sends[0, q, peer]]
            halo_copy(pools, parity, h, peer, me).start()

        for q in range(slots):
            pools[h][blocks + me * slots + q] = fresh[h][sends[0, q, me]]

    def finish_halo(pools, parity, h):
        @pl.loop(1, parts)
        def _(d):
            peer = lax.rem(me + d, parts)
            halo_copy(pools, parity, h, me, peer).wait_recv()

        @pl.loop(1, parts)
        def _(d):
            peer = lax.rem(me + d, parts)
            halo_copy(pools, parity, h, peer, me).wait_send()

    def start_cut(piece, one, two):
        for n in range(narrow):
            span = slice(n * share, (n + 1) * share)
            cut[piece, n] = jnp.concatenate([one[:, span], two[:, span]], axis=1).astype(bf16)

        @pl.loop(1, narrow)
        def _(d):
            peer = lax.rem(mine + d, narrow)
            cut_copy(piece, peer, mine).start()

        land[piece, pl.ds(mine * width, width), :] = cut[piece, mine]

    def apply(pool, b):
        left = jnp.concatenate([pool[lists[k, b]] for k in range(fan)], axis=1)
        summed = dot(left, tiles[b])
        return (summed / degree[pl.ds(b, 1), :]).astype(bf16)

    for h in range(2):
        start_halo(pool_a, 0, h)

    @pl.loop(1, parts)
    def _(d):
        peer = lax.rem(me + d, parts)
        count_copy(peer, me).start()

    step = onehot.shape[0] // blocks

    @pl.loop(0, blocks)
    def _(b):
        start = pl.multiple_of(b * step, step)
        node = lax.broadcasted_iota(jnp.int32, (step, rows), 0) + start
        onehot[pl.ds(start, step), :] = jnp.where(node == ids[...], 1.0, 0.0).astype(bf16)

    picked[0] = dot(feat[...], onehot[...])
    load.wait()

    @pl.loop(0, blocks)
    def _(b):
        degree[pl.ds(b, 1), :] = jnp.sum(tiles[b].astype(f32), axis=0, keepdims=True)

    cnt_buf[me] = cnt[...]

    @pl.loop(1, parts)
    def _(d):
        peer = lax.rem(me + d, parts)
        count_copy(me, peer).wait_recv()

    counts = jnp.sum(cnt_buf[...], axis=0)[:, 0:1]
    scale = jnp.sum(named * (1.0 / jnp.maximum(counts, 1.0)), axis=0, keepdims=True)
    for pair in range(2):
        start_cut(
            pair,
            cot[2 * pair].astype(f32) * scale,
            cot[2 * pair + 1].astype(f32) * scale,
        )

    unroll = 4

    @pl.loop(0, HOPS)
    def _(hop):
        for h in range(2):
            finish_halo(pool_a, 0, h)

            @pl.loop(0, blocks, step=unroll)
            def _(b):
                for c in range(unroll):
                    once = apply(pool_a[h], b + c)
                    pool_b[h][b + c] = once
                    fresh[h][b + c] = once

            start_halo(pool_b, 1, h)

        for h in range(2):
            finish_halo(pool_b, 1, h)

            @pl.loop(0, blocks, step=unroll)
            def _(b):
                for c in range(unroll):
                    twice = apply(pool_b[h], b + c).astype(f32)
                    smooth = 0.5 * pool_a[h][b + c].astype(f32) + pool_b[h][b + c].astype(f32)
                    smooth = (smooth + twice).astype(bf16)
                    pool_a[h][b + c] = smooth
                    fresh[h][b + c] = smooth
                    start = pl.multiple_of((b + c) * LANES, LANES)
                    hops_out[hop, h * half:(h + 1) * half, pl.ds(start, LANES)] = smooth

            @pl.when(hop < HOPS - 1)
            def _():
                start_halo(pool_a, 0, h)

        picked[hop + 1] = dot(hops_out[hop], onehot[...])

        @pl.when(hop == 0)
        def _():
            start_cut(2, picked[0], picked[1])

    start_cut(3, picked[2], picked[3])

    @pl.loop(1, parts)
    def _(d):
        peer = lax.rem(me + d, parts)
        count_copy(peer, me).wait_send()

    for piece in range(TOKS):
        @pl.loop(1, narrow)
        def _(d):
            peer = lax.rem(mine + d, narrow)
            cut_copy(piece, mine, peer).wait_recv()
            cut_copy(piece, peer, mine).wait_send()

    packed_out[...] = land[...]


def smooth_hops(
    parts, narrow, features, edge_tiles, block_lists, send_lists, train_ids, owners, cotangent
):
    width, nodes = features.shape
    blocks, fan, size, _ = edge_tiles.shape
    slots = send_lists.shape[2]
    rows = train_ids.shape[0]
    pool = blocks + parts * slots
    half = width // 2
    devices = -(-parts * narrow // 8) * 8
    lanes = 2 * rows // narrow
    vmem = pl.BlockSpec(memory_space=pltpu.VMEM)
    smem = pl.BlockSpec(memory_space=pltpu.SMEM)
    return pl.pallas_call(
        functools.partial(hop_kernel, parts, narrow),
        out_shape=(
            jax.ShapeDtypeStruct((HOPS, width, nodes), bf16),
            jax.ShapeDtypeStruct((TOKS, width * narrow, lanes), bf16),
        ),
        in_specs=[smem, smem, vmem, pl.BlockSpec(memory_space=pl.ANY), vmem, vmem, vmem],
        out_specs=(vmem, vmem),
        scratch_shapes=[pltpu.VMEM((pool, half, size), bf16)] * 4
        + [pltpu.VMEM((blocks, half, size), bf16)] * 2
        + [pltpu.VMEM((parts, slots, half, size), bf16)] * 2
        + [
            pltpu.VMEM((blocks, fan * size, size), bf16),
            pltpu.VMEM((blocks, size), f32),
            pltpu.VMEM((nodes, rows), bf16),
            pltpu.VMEM((devices, LANES), f32),
            pltpu.VMEM((parts, devices, LANES), f32),
            pltpu.VMEM((TOKS, width, rows), f32),
            pltpu.VMEM((TOKS, narrow, width, lanes), bf16),
            pltpu.VMEM((TOKS, width * narrow, lanes), bf16),
            pltpu.SemaphoreType.DMA,
            pltpu.SemaphoreType.DMA((2, parts)),
            pltpu.SemaphoreType.DMA((4, parts)),
            pltpu.SemaphoreType.DMA((parts,)),
            pltpu.SemaphoreType.DMA((parts,)),
            pltpu.SemaphoreType.DMA((TOKS, narrow)),
            pltpu.SemaphoreType.DMA((TOKS, narrow)),
        ],
        compiler_params=pltpu.CompilerParams(
            collective_id=0, has_side_effects=True, vmem_limit_bytes=56 * 2**20
        ),
        name="smooth_hops",
    )(
        block_lists.T, send_lists.transpose(0, 2, 1), features,
        edge_tiles.reshape(blocks, fan * size, size),
        train_ids.reshape(1, rows), owners.reshape(1, rows), cotangent,
    )


def normalize(hidden):
    center = hidden - jnp.mean(hidden, axis=0, keepdims=True)
    inverse = lax.rsqrt(jnp.mean(center * center, axis=0, keepdims=True) + EPSILON)
    return center * inverse, inverse


def layer_kernel(
    bits, orders, packed, wq, wk, wv, wo, wu, wd, attn_out, up_out, down_out,
    nb_ref, cot_ref, g_ref, attn_sum, up_sum, down_sum, attn_in, up_in, down_in,
    send_sem, recv_sem,
):
    outs = (attn_out, up_out, down_out)
    terms = (attn_sum, up_sum, down_sum)
    incoming = (attn_in, up_in, down_in)
    devices, piece = attn_sum.shape[:2]
    stages = len(bits)
    me = [lax.axis_index(axis) for axis, _, _ in bits]
    own = [lax.rem(lax.div(i, 1 << shift), 2) for i, (_, shift, _) in zip(me, bits)]
    partner = [
        {axis: i + (1 - 2 * m) * (1 << shift)} for i, m, (axis, shift, _) in zip(me, own, bits)
    ]
    barrier = pltpu.get_barrier_semaphore()
    for peer in partner:
        pl.semaphore_signal(barrier, inc=1, device_id=peer, device_id_type=MESH)
    pl.semaphore_wait(barrier, stages)

    def place(chain, block):
        spot = 0
        for bit in orders[chain]:
            weight = bits[bit][2]
            if isinstance(block, int):
                spot = 2 * spot + block // weight % 2
            else:
                spot = 2 * spot + lax.rem(lax.div(block, weight), 2)
        return spot

    def put(chain, first, value):
        value = value.astype(bf16)
        for c in range(value.shape[0] // piece):
            terms[chain][place(chain, first + c)] = value[c * piece:(c + 1) * piece, :]

    bases = [[0], [0], [0]]

    def exchange(chain, stage):
        bit = orders[chain][stage]
        half = devices >> (stage + 1)
        base = bases[chain][stage]
        if len(bases[chain]) == stage + 1:
            bases[chain].append(base + own[bit] * half)
        return pltpu.make_async_remote_copy(
            src_ref=terms[chain].at[pl.ds(base + (1 - own[bit]) * half, half)],
            dst_ref=incoming[chain].at[pl.ds(devices - 2 * half, half)],
            send_sem=send_sem.at[chain, stage],
            recv_sem=recv_sem.at[chain, stage],
            device_id=partner[bit],
            device_id_type=MESH,
        )

    def absorb(chain, stage):
        exchange(chain, stage).wait_recv()
        half = devices >> (stage + 1)
        base = bases[chain][stage + 1]

        if stage == stages - 1:
            outs[chain][...] = (
                terms[chain][base].astype(f32) + incoming[chain][devices - 2].astype(f32)
            )
        else:
            @pl.loop(0, half)
            def _(i):
                total = terms[chain][base + i].astype(f32)
                total = total + incoming[chain][devices - 2 * half + i].astype(f32)
                terms[chain][base + i] = total.astype(bf16)

            exchange(chain, stage + 1).start()

    share = packed.shape[2] // 2
    width = packed.shape[1]
    cols = TOKS * share
    head = width // HEADS
    scale = 1.0 / math.sqrt(head)
    cot32 = jnp.concatenate([packed[t].astype(f32) for t in range(2)], axis=1)
    x = jnp.concatenate([packed[2 + t].astype(f32) for t in range(2)], axis=1)
    cot_ref[...] = cot32.astype(bf16)

    def ahead(v, j):
        return v if j == 0 else pltpu.roll(v, cols - j * share, 1)

    def back(v, j):
        return v if j == 0 else pltpu.roll(v, j * share, 1)

    def head_sum(v):
        return jnp.sum(v.reshape(HEADS, head, cols), axis=1)

    def spread(v):
        return jnp.broadcast_to(v[:, None, :], (HEADS, head, cols)).reshape(width, cols)

    def low(v):
        return v.astype(bf16).astype(f32)

    normed_a = normalize(x)[0].astype(bf16)
    query = low(dot(wq[...], normed_a))
    key = low(dot(wk[...], normed_a))
    value = low(dot(wv[...], normed_a))
    scores = [head_sum(query * ahead(key, j)) * scale for j in range(TOKS)]
    top = functools.reduce(jnp.maximum, scores)
    exps = [jnp.exp(s - top) for s in scores]
    total = functools.reduce(jnp.add, exps)
    probs = [e / total for e in exps]
    probs_low = [low(p) for p in probs]
    mixed = functools.reduce(
        jnp.add, [spread(probs_low[j]) * ahead(value, j) for j in range(TOKS)]
    ).astype(bf16)
    residual = low(x + dot(wo[...], mixed))
    second, inverse = normalize(residual)
    nb_ref[...] = second.astype(bf16)
    g_ref[...] = jnp.zeros_like(g_ref)
    chunk = 256
    slope = math.sqrt(2.0 / math.pi)

    @pl.loop(0, wu.shape[0] // chunk)
    def _(i):
        rows = pl.ds(pl.multiple_of(i * chunk, chunk), chunk)
        up = wu[rows, :]
        cot = cot_ref[...]
        normed_b = nb_ref[...]
        pre = dot(up, normed_b)
        square = pre * pre
        tanh = jnp.tanh(slope * (pre + 0.044715 * (square * pre)))
        activated = (0.5 * pre * (1.0 + tanh)).astype(bf16)
        deriv = 0.5 * (1.0 + tanh) + 0.5 * pre * (1.0 - tanh * tanh) * (
            slope * (1.0 + 3.0 * 0.044715 * square)
        )
        put(2, i * (chunk // piece), dot(activated, cot, NT))
        grad_pre = (dot(wd[rows, :], cot) * deriv).astype(bf16)
        put(1, i * (chunk // piece), dot(grad_pre, normed_b, NT))
        g_ref[...] += dot(up, grad_pre, TN)

    exchange(2, 0).start()
    exchange(1, 0).start()
    group = width // piece
    upstream = g_ref[...]
    grad_resid = (
        cot32
        + inverse
        * (
            upstream
            - jnp.mean(upstream, axis=0, keepdims=True)
            - second * jnp.mean(upstream * second, axis=0, keepdims=True)
        )
    ).astype(bf16)
    put(0, 3 * group, dot(grad_resid, mixed, NT))
    grad_mixed = low(dot(wo[...], grad_resid, TN))
    grad_probs = [head_sum(grad_mixed * ahead(value, j)) for j in range(TOKS)]
    grad_value = functools.reduce(
        jnp.add, [back(spread(probs_low[j]) * grad_mixed, j) for j in range(TOKS)]
    ).astype(bf16)
    put(0, 2 * group, dot(grad_value, normed_a, NT))
    inner = functools.reduce(jnp.add, [p * g for p, g in zip(probs, grad_probs)])
    grad_scores = [low(p * (g - inner) * scale) for p, g in zip(probs, grad_probs)]
    grad_query = functools.reduce(
        jnp.add, [spread(grad_scores[j]) * ahead(key, j) for j in range(TOKS)]
    ).astype(bf16)
    put(0, 0, dot(grad_query, normed_a, NT))
    grad_key = functools.reduce(
        jnp.add, [back(spread(grad_scores[j]) * query, j) for j in range(TOKS)]
    ).astype(bf16)
    put(0, group, dot(grad_key, normed_a, NT))
    exchange(0, 0).start()
    for stage in range(stages):
        for chain in (2, 1, 0):
            absorb(chain, stage)
    for chain in range(3):
        for stage in range(stages):
            exchange(chain, stage).wait_send()


def layer_sums(parts, narrow, packed, wq, wk, wv, wo, wu, wd):
    width = packed.shape[1]
    cols = 2 * packed.shape[2]
    devices = parts * narrow
    piece = wu.shape[0] // devices
    bits = [("narrow", s, 1 << s) for s in range(narrow.bit_length() - 1)]
    bits += [("wide", s, narrow << s) for s in range(parts.bit_length() - 1)]
    near, far = list(range(1, min(4, len(bits)))), list(range(4, len(bits)))
    orders = [[0] + near[c:] + near[:c] + far for c in range(3)]
    vmem = pl.BlockSpec(memory_space=pltpu.VMEM)
    return pl.pallas_call(
        functools.partial(layer_kernel, bits, orders),
        out_shape=(jax.ShapeDtypeStruct((piece, width), f32),) * 3,
        in_specs=[vmem] * 7,
        out_specs=(vmem, vmem, vmem),
        scratch_shapes=[
            pltpu.VMEM((width, cols), bf16),
            pltpu.VMEM((width, cols), bf16),
            pltpu.VMEM((width, cols), f32),
        ]
        + [pltpu.VMEM((devices, piece, width), bf16)] * 6
        + [pltpu.SemaphoreType.DMA((3, len(bits)))] * 2,
        compiler_params=pltpu.CompilerParams(
            collective_id=1, has_side_effects=True, vmem_limit_bytes=48 * 2**20
        ),
        name="layer_sums",
    )(packed, wq, wk, wv, wo, wu, wd)


def on_device(
    features, edge_tiles, block_lists, send_lists, train_ids, owners, cotangent,
    query_weight, key_weight, value_weight, out_weight, up_weight, down_weight,
):
    parts = lax.axis_size("wide")
    narrow = lax.axis_size("narrow")
    hop_tokens, packed = smooth_hops(
        parts, narrow, features, edge_tiles, block_lists, send_lists, train_ids, owners, cotangent
    )
    sums = layer_sums(
        parts, narrow, packed,
        query_weight, key_weight, value_weight, out_weight, up_weight, down_weight,
    )
    return (hop_tokens, *sums)


def solution(mesh):
    in_specs = (
        P("narrow", "wide"),
        P("wide", None, None, None),
        P("wide", None),
        P("wide", None, None),
        P("wide"),
        P("wide", None),
        P(None, "narrow", "wide"),
        P(),
        P(),
        P(),
        P(),
        P(),
        P(),
    )
    out_specs = (
        P(None, "narrow", "wide"),
        P(("wide", "narrow"), None),
        P(("wide", "narrow"), None),
        P(("wide", "narrow"), None),
    )
    return jax.shard_map(
        on_device, mesh=mesh, in_specs=in_specs, out_specs=out_specs, check_vma=False
    )
```
